512 devices in a mesh: loop: 32 (over z, y_hi), rep: 4 (over x), feat: 4 (over y_lo, core).
Axes of the slice: x: 4, y: 4 (y_hi: 2, y_lo: 2; y = y_hi * 2 + y_lo), z: 16, core: 2. Of those that a mesh axis runs over, the one named last changes fastest.
Arguments:
- features: bfloat16 [128, 32768], P('feat', 'loop'), may hold values from -6 to 6
- tile_values: bfloat16 [32, 4, 112, 128, 128], P('loop', 'rep'), may hold values from -0.1875 to 0.1875
- tile_coords: int32 [32, 4, 2, 112], P('loop', 'rep'), may hold values from 0 to 7, as said below
- section_counts: int32 [32, 4, 8], P('loop', 'rep'), may hold values from 0 to 64, as said below
- weight_one: bfloat16 [128, 128], replicated, may hold values from -0.5 to 0.5
- weight_two: bfloat16 [128, 128], replicated, may hold values from -0.5 to 0.5
- cotangent: bfloat16 [128, 32768], P(None, ('loop', 'feat')), may hold values from -24 to 24
Outputs:
- grad_one: float32 [128, 128], replicated
- grad_two: float32 [128, 128], replicated
- input_grad: bfloat16 [128, 32768], P('feat', 'loop')
The draws below stay inside these ranges and needn't reach their ends.
Inputs may be any that keep to these rules, and one draw needn't show every extreme that they name: `tile_coords`: slots of a list are grouped by section in order of sections; the live slots of one section name distinct (row, column) pairs; slots past the list's total count hold 0. `section_counts`: section k of rep index r covers the column block r + 4 * k places below the list's own loop index; sections with r + 4 * k of 32 or more hold 0.
All inputs are finite; a program needn't handle non-finite values.
Results may differ from the reference program's by a relative error of at most 0.029.
Values may be sent and summed in bfloat16 or wider, within the bound.
A program may use at most 64 MiB of HBM per device.

```python
import math
import jax
import jax.numpy as jnp
from jax import lax

D = 128
TILE = 128
PANELS = 8
LOOPS = 32
REPLICAS = 4
SECTIONS = 8
TILE_DEV = 112
NODES = 32768


def tile_plan(key):
    base_key = jax.random.fold_in(key, 7)
    rep_ids = jnp.arange(REPLICAS, dtype=jnp.int32)[None, :, None]
    section_ids = jnp.arange(SECTIONS, dtype=jnp.int32)[None, None, :]
    offset = rep_ids + REPLICAS * section_ids
    distance = jnp.minimum(offset, LOOPS - offset)
    ceiling = jnp.minimum(40 // jnp.maximum(distance, 1), PANELS * PANELS)
    drawn = jax.random.randint(jax.random.fold_in(base_key, 1), (LOOPS, REPLICAS, SECTIONS), 0, ceiling + 1)
    counts = jnp.where(distance == 0, PANELS * PANELS, drawn)
    counts = jnp.where(offset >= LOOPS, 0, counts).astype(jnp.int32)
    pair_count = PANELS * PANELS
    scores = jax.random.randint(jax.random.fold_in(base_key, 2), (LOOPS, REPLICAS, SECTIONS, pair_count), 0, 2 ** 20)
    scores = scores * pair_count + jnp.arange(pair_count, dtype=jnp.int32)
    orders = jnp.argsort(scores, axis=-1).astype(jnp.int32)
    ends = jnp.cumsum(counts, axis=-1)
    starts = ends - counts
    slot_ids = jnp.arange(TILE_DEV, dtype=jnp.int32)
    section_of = jnp.sum((slot_ids[None, None, :, None] >= ends[:, :, None, :]).astype(jnp.int32), axis=-1)
    section_of = jnp.minimum(section_of, SECTIONS - 1)
    begin = jnp.take_along_axis(starts, section_of, axis=2)
    within = jnp.clip(slot_ids[None, None, :] - begin, 0, pair_count - 1)
    alive = slot_ids[None, None, :] < ends[:, :, -1:]
    flat_orders = orders.reshape(LOOPS, REPLICAS, SECTIONS * pair_count)
    pairs = jnp.take_along_axis(flat_orders, section_of * pair_count + within, axis=2)
    pairs = jnp.where(alive, pairs, 0)
    coords = jnp.stack([pairs // PANELS, pairs % PANELS], axis=2).astype(jnp.int32)
    return (counts, coords)


def draw_tile_coords(key, part):
    return tile_plan(key)[1]


def draw_section_counts(key, part):
    return tile_plan(key)[0]


def draw_cotangent(key, part):
    position = jnp.arange(NODES, dtype=jnp.float32) / max(NODES - 1, 1)
    rising = 1.0 + 2.0 * position
    value = jax.random.normal(key, (D, NODES), jnp.float32) * rising[None, :]
    return jnp.clip(value, -24.0, 24.0).astype(jnp.bfloat16)


def levels(stream_key, extent, cuts, smallest, high):
    factor_of = 1.0
    for dim, parts in cuts:
        heights = jax.random.uniform(jax.random.fold_in(jax.random.fold_in(stream_key, 6), dim), (parts,), jnp.float32, smallest / len(cuts), high / len(cuts))
        factor_of = factor_of * jnp.repeat(jnp.exp(heights), extent[dim] // parts).reshape((-1,) + (1,) * (len(extent) - 1 - dim))
    return factor_of


def scatter_about(own_key, dims, spread, reach, shards=(), kind=jnp.bfloat16):
    entries = spread * jax.random.normal(own_key, dims, jnp.float32)
    if shards:
        entries = entries * levels(own_key, dims, shards, -0.22, 0.18)
    return jnp.clip(entries, -reach, reach).astype(kind)


def setup_inputs(seed: int = 0) -> dict:
    seeds = jax.random.split(jax.random.key(seed), 8)
    return {
        "features": scatter_about(seeds[0], (D, NODES), 1.0, 6.0, ((0, 4), (1, 32))),
        "tile_values": scatter_about(seeds[1], (LOOPS, REPLICAS, TILE_DEV, TILE, TILE), (PANELS * TILE) ** -0.5, 0.1875, ((0, 32), (1, 4))),
        "tile_coords": draw_tile_coords(jax.random.fold_in(seeds[7], 71), 0),
        "section_counts": draw_section_counts(jax.random.fold_in(seeds[7], 71), 0),
        "weight_one": scatter_about(seeds[4], (D, D), D ** -0.5, 0.5),
        "weight_two": scatter_about(seeds[5], (D, D), D ** -0.5, 0.5),
        "cotangent": draw_cotangent(jax.random.fold_in(seeds[7], 71), 0),
    }


def slot_plan(tile_coords, section_counts):
    ends = jnp.cumsum(section_counts, axis=-1)
    slot_ids = jnp.arange(TILE_DEV, dtype=jnp.int32)
    section_ids = lax.optimization_barrier(jnp.sum((slot_ids[None, None, :, None] >= ends[:, :, None, :]).astype(jnp.int32), axis=-1))
    alive = slot_ids[None, None, :] < ends[:, :, -1:]
    section_ids = jnp.minimum(section_ids, SECTIONS - 1)
    loop_ids = jnp.arange(LOOPS, dtype=jnp.int32)[:, None, None]
    rep_ids = jnp.arange(REPLICAS, dtype=jnp.int32)[None, :, None]
    block_ids = jnp.mod(loop_ids - rep_ids - REPLICAS * section_ids, LOOPS)
    row_panels = tile_coords[:, :, 0, :]
    col_panels = block_ids * PANELS + tile_coords[:, :, 1, :]
    return (row_panels, col_panels, alive)

def apply_forward(source, tile_values, row_panels, col_panels, alive):
    width = source.shape[0]
    pieces = source.reshape(width, LOOPS * PANELS, TILE).transpose(1, 0, 2)
    panel_ids = jnp.arange(PANELS, dtype=jnp.int32)

    def one_loop(index):
        tiles_here = tile_values[index].reshape(-1, TILE, TILE).astype(jnp.float32)
        cols_here = col_panels[index].reshape(-1)
        rows_here = row_panels[index].reshape(-1)
        alive_here = alive[index].reshape(-1)
        picked = pieces[cols_here].astype(jnp.float32)
        products = jnp.einsum('bdc,bac->bda', picked, tiles_here, precision=lax.Precision.HIGHEST)
        placing = ((rows_here[:, None] == panel_ids[None, :]) & alive_here[:, None]).astype(jnp.float32)
        return jnp.einsum('bda,bp->dpa', products, placing, precision=lax.Precision.HIGHEST)
    blocks = lax.map(one_loop, jnp.arange(LOOPS, dtype=jnp.int32))
    return blocks.transpose(1, 0, 2, 3).reshape(width, NODES)

def apply_transposed(source, tile_values, row_panels, col_panels, alive):
    width = source.shape[0]
    pieces = source.reshape(width, LOOPS * PANELS, TILE).transpose(1, 0, 2)

    def one_loop(index, running):
        tiles_here = tile_values[index].reshape(-1, TILE, TILE).astype(jnp.float32)
        cols_here = col_panels[index].reshape(-1)
        rows_here = index * PANELS + row_panels[index].reshape(-1)
        alive_here = alive[index].reshape(-1).astype(jnp.float32)
        picked = pieces[rows_here].astype(jnp.float32)
        products = jnp.einsum('bda,bac->bdc', picked, tiles_here, precision=lax.Precision.HIGHEST)
        products = products * alive_here[:, None, None]
        return running.at[cols_here].add(products)
    start_sum = jnp.zeros((LOOPS * PANELS, width, TILE), jnp.float32)
    running = lax.fori_loop(0, LOOPS, one_loop, start_sum)
    return running.transpose(1, 0, 2).reshape(width, NODES)

def silu_slope(value):
    sigmoid_value = jax.nn.sigmoid(value)
    return sigmoid_value * (1.0 + value * (1.0 - sigmoid_value))

def reference(features, tile_values, tile_coords, section_counts, weight_one, weight_two, cotangent):
    row_panels, col_panels, alive = slot_plan(tile_coords, section_counts)
    scale = 1.0 / math.sqrt(NODES)
    mix_one = apply_forward(features, tile_values, row_panels, col_panels, alive).astype(jnp.bfloat16)
    z_one = jnp.dot(weight_one.T, mix_one, preferred_element_type=jnp.float32)
    h_one = jax.nn.silu(z_one).astype(jnp.bfloat16)
    mix_two = apply_forward(h_one, tile_values, row_panels, col_panels, alive).astype(jnp.bfloat16)
    z_two = jnp.dot(weight_two.T, mix_two, preferred_element_type=jnp.float32)
    dz_two = (cotangent * silu_slope(z_two)).astype(jnp.bfloat16)
    grad_two = jnp.dot(mix_two, dz_two.T, preferred_element_type=jnp.float32) * scale
    dm_two = jnp.dot(weight_two, dz_two, preferred_element_type=jnp.float32).astype(jnp.bfloat16)
    dh_one = apply_transposed(dm_two, tile_values, row_panels, col_panels, alive).astype(jnp.bfloat16)
    dz_one = (dh_one * silu_slope(z_one)).astype(jnp.bfloat16)
    grad_one = jnp.dot(mix_one, dz_one.T, preferred_element_type=jnp.float32) * scale
    dm_one = jnp.dot(weight_one, dz_one, preferred_element_type=jnp.float32).astype(jnp.bfloat16)
    input_grad = apply_transposed(dm_one, tile_values, row_panels, col_panels, alive).astype(jnp.bfloat16)
    return (grad_one, grad_two, input_grad)
```

```python
import functools
import math

import jax
import jax.numpy as jnp
from jax import lax
from jax.experimental import pallas as pl
from jax.experimental.pallas import tpu as pltpu
from jax.sharding import PartitionSpec as P

MESH = pl.DeviceIdType.MESH
BF16 = jnp.bfloat16
F32 = jnp.float32


def place_kernel(row_ids, col_ids, starts, ends, tiles, out):
    section = pl.program_id(0)
    side = tiles.shape[-1]
    per_chunk = out.shape[-1] // side
    out[...] = jnp.zeros_like(out)

    def one_tile(slot, carry):
        row = pl.multiple_of(row_ids[slot] * side, side)
        col = col_ids[slot]
        lane = pl.multiple_of(lax.rem(col, per_chunk) * side, side)
        out[0, lax.div(col, per_chunk), pl.ds(row, side), pl.ds(lane, side)] = tiles[slot]
        return carry

    lax.fori_loop(starts[section], ends[section], one_tile, 0)


def dense_sections(tile_set, row_ids, col_ids, starts, ends, chunks, nodes):
    sections = starts.shape[0]
    width = nodes // chunks
    return pl.pallas_call(
        place_kernel,
        out_shape=jax.ShapeDtypeStruct((sections, chunks, nodes, width), BF16),
        grid_spec=pltpu.PrefetchScalarGridSpec(
            num_scalar_prefetch=4,
            grid=(sections,),
            in_specs=[pl.BlockSpec(tile_set.shape, lambda k, *_: (0, 0, 0))],
            out_specs=pl.BlockSpec((1, chunks, nodes, width), lambda k, *_: (k, 0, 0, 0)),
        ),
        name="place_tiles",
    )(row_ids, col_ids, starts, ends, tile_set)


def nt_dot(a, b):
    return lax.dot_general(a, b, (((1,), (1,)), ((), ())), preferred_element_type=F32)


def nn_dot(a, b):
    return lax.dot_general(a, b, (((1,), (0,)), ((), ())), preferred_element_type=F32)


def slope_of(z):
    s = 1.0 / (1.0 + jnp.exp(-z))
    return s * (1.0 + z * (1.0 - s))


def layers_kernel(
    sizes,
    feat_ref, dense_hbm, w1, w1t, w2, w2t, cot_ref,
    out_ref, g1_ref, g2_ref,
    dense, hbuf, acc, pst, ebuf, fin, lst, dmb, dmf, z1, mix, rd, ru, sd, su,
    asem, ringr, fs, bs, xs, xr, ls, dmr, p0s, rdr, rur, ds, us,
):
    L, R, F = sizes
    S = L // R
    H = S // 2
    half = F // 2
    C = hbuf.shape[-1]
    i, r, f = lax.axis_index("loop"), lax.axis_index("rep"), lax.axis_index("feat")

    def at_loop(value):
        return lax.rem(value + L, L)

    up, dn = at_loop(i + R), at_loop(i - R)
    ahead, behind = at_loop(i + r), at_loop(i - r)

    def local(src, dst, sem):
        return pltpu.make_async_copy(src, dst, sem)

    def remote(src, dst, ssem, rsem, to):
        return pltpu.make_async_remote_copy(
            src_ref=src, dst_ref=dst, send_sem=ssem, recv_sem=rsem,
            device_id=to, device_id_type=MESH,
        )

    def done(ref, sem):
        pltpu.make_async_copy(ref, ref, sem).wait()

    order = [0]
    for s in range(1, H):
        order += [s, S - s]
    order += [H]
    for k in order:
        local(dense_hbm.at[k], dense.at[k], asem.at[k]).start()

    barrier = pltpu.get_barrier_semaphore()

    def greet(*to):
        pl.semaphore_signal(barrier, inc=1, device_id=to, device_id_type=MESH)

    greet(up, r, f)
    greet(dn, r, f)
    for a in range(R):
        for b in range(F):
            if (a, b) != (0, 0):
                greet(i, lax.rem(r + a, R), lax.rem(f + b, F))

    @pl.when(r != 0)
    def _():
        for b in range(F):
            greet(behind, r, b)

    for a in range(1, R):
        for b in range(F):
            greet(at_loop(i + a), a, b)
    zero = jnp.zeros(rd.shape[3:], BF16)
    for p in range(2):
        for q in range(F):
            if q >= half:
                rd[p, 0, q] = zero
            else:
                ru[p, 0, q] = zero
    pl.semaphore_wait(barrier, 1 + R * F + jnp.where(r != 0, F + R * F, 0))

    for q in range(F):
        src = feat_ref.at[:, pl.ds(q * C, C)]

        @pl.when(r == 0)
        def _():
            local(src, hbuf.at[0, 0, q], ringr.at[0, 0, q]).start()

        @pl.when(r != 0)
        def _():
            remote(src, hbuf.at[0, 0, q], p0s.at[q], ringr.at[0, 0, q], (ahead, r, f)).start()

    def forward(p):
        def send_up(k, q):
            return remote(hbuf.at[p, k, q], hbuf.at[p, k + 1, q], fs.at[p, k, q], ringr.at[p, k + 1, q], (up, r, f))

        def send_dn(k, s, q):
            to = S - 1 - s
            return remote(hbuf.at[p, k, q], hbuf.at[p, to, q], bs.at[p, s, q], ringr.at[p, to, q], (dn, r, f))

        def term(k, q):
            return nt_dot(hbuf[p, k, q], dense[k, q])

        if p == 0:
            done(dense.at[0], asem.at[0])

        def first(q, carry):
            done(hbuf.at[p, 0, q], ringr.at[p, 0, q])
            send_up(0, q).start()
            send_dn(0, 0, q).start()

            @pl.when(q == 0)
            def _():
                acc[...] = term(0, q)

            @pl.when(q != 0)
            def _():
                acc[...] += term(0, q)

            return carry

        lax.fori_loop(0, F, first, 0)

        def stage(s, carry):
            kb = S - s
            if p == 0:
                done(dense.at[s], asem.at[s])
                done(dense.at[kb], asem.at[kb])

            def chunk(q, inner):
                done(hbuf.at[p, s, q], ringr.at[p, s, q])

                @pl.when((s < H - 1) | (q < half))
                def _():
                    send_up(s, q).start()

                done(hbuf.at[p, kb, q], ringr.at[p, kb, q])

                @pl.when((s < H - 1) | (q >= half))
                def _():
                    send_dn(kb, s, q).start()

                acc[...] += term(s, q) + term(kb, q)
                return inner

            return lax.fori_loop(0, F, chunk, carry)

        lax.fori_loop(1, H, stage, 0)
        if p == 0:
            done(dense.at[H], asem.at[H])

        def last(q, carry):
            done(hbuf.at[p, H, q], ringr.at[p, H, q])
            acc[...] += term(H, q)
            return carry

        lax.fori_loop(0, F, last, 0)
        for q in range(F):
            pst[p, q] = acc[:, q * C:(q + 1) * C].astype(BF16)
        for a in range(R):
            for b in range(F):
                rr, q = lax.rem(r + a, R), lax.rem(f + b, F)
                if (a, b) == (0, 0):
                    local(pst.at[p, q], ebuf.at[p, r, f], xr.at[p, r, f]).start()
                else:
                    remote(pst.at[p, q], ebuf.at[p, r, f], xs.at[p, a, b], xr.at[p, r, f], (i, rr, q)).start()

    def gathered(e):
        total = None
        for a in range(R):
            for b in range(F):
                done(ebuf.at[e, a, b], xr.at[e, a, b])
        for a in range(R):
            part = ebuf[e, a].reshape(z1.shape).astype(F32)
            total = part if total is None else total + part
        return total.astype(BF16)

    def spread(n, value, to_loop, dst, sem, shifted):
        lst[n] = value.reshape(lst.shape[1:])
        for b in range(F):
            ff = lax.rem(f + b, F)

            def away():
                remote(lst.at[n, ff], dst.at[f], ls.at[n, ff], sem.at[f], (to_loop, r, ff)).start()

            def here():
                local(lst.at[n, ff], dst.at[f], sem.at[f]).start()

            if b:
                away()
            elif shifted:
                pl.when(r == 0)(here)
                pl.when(r != 0)(away)
            else:
                here()

    def transposed(p):
        for q in range(F):
            done(dmb.at[p, q], dmr.at[p, q])
            dmf[:, q * C:(q + 1) * C] = dmb[p, q]

        def send_dn(s, q):
            return remote(sd.at[p, s, q], rd.at[p, s, q], ds.at[p, s, q], rdr.at[p, s, q], (dn, r, f))

        def send_up(s, q):
            return remote(su.at[p, s, q], ru.at[p, s, q], us.at[p, s, q], rur.at[p, s, q], (up, r, f))

        def first(q, carry):
            value = nn_dot(dmf[...], dense[H, q]).astype(BF16)

            @pl.when(q < half)
            def _():
                sd[p, 0, q] = value
                send_dn(0, q).start()

            @pl.when(q >= half)
            def _():
                su[p, 0, q] = value
                send_up(0, q).start()

            return carry

        lax.fori_loop(0, F, first, 0)

        def stage(s, carry):
            def chunk(q, inner):
                down = nn_dot(dmf[...], dense[H - s, q])
                above = nn_dot(dmf[...], dense[H + s, q])

                @pl.when((s > 1) | (q < half))
                def _():
                    done(rd.at[p, s - 1, q], rdr.at[p, s - 1, q])

                sd[p, s, q] = (down + rd[p, s - 1, q].astype(F32)).astype(BF16)
                send_dn(s, q).start()

                @pl.when((s > 1) | (q >= half))
                def _():
                    done(ru.at[p, s - 1, q], rur.at[p, s - 1, q])

                su[p, s, q] = (above + ru[p, s - 1, q].astype(F32)).astype(BF16)
                send_up(s, q).start()
                return inner

            return lax.fori_loop(0, F, chunk, carry)

        lax.fori_loop(1, H, stage, 0)
        x = 2 + p

        def last(q, carry):
            own = nn_dot(dmf[...], dense[0, q])
            done(rd.at[p, H - 1, q], rdr.at[p, H - 1, q])
            done(ru.at[p, H - 1, q], rur.at[p, H - 1, q])
            own = own + rd[p, H - 1, q].astype(F32) + ru[p, H - 1, q].astype(F32)
            pst[x, q] = own.astype(BF16)
            for a in range(R):
                rr = lax.rem(r + a, R)
                if p == 0:
                    dst, sem, to, mine = ebuf.at[2, r, f], xr.at[2, r, f], (behind, rr, q), (r == 0) & (q == f)
                else:
                    dst, sem, to, mine = fin.at[r, q], xr.at[3, r, q], (behind, rr, f), r == 0

                def away():
                    remote(pst.at[x, q], dst, xs.at[x, a, q], sem, to).start()

                if a:
                    away()
                else:
                    pl.when(mine)(lambda: local(pst.at[x, q], dst, sem).start())
                    pl.when(jnp.logical_not(mine))(away)
            return carry

        lax.fori_loop(0, F, last, 0)

    forward(0)
    mix_one = gathered(0)
    mix[0] = mix_one
    z_one = nn_dot(w1t[...], mix_one)
    z1[...] = z_one
    h_one = (z_one / (1.0 + jnp.exp(-z_one))).astype(BF16)
    spread(0, h_one, ahead, hbuf.at[1, 0], ringr.at[1, 0], True)
    forward(1)
    mix_two = gathered(1)
    mix[1] = mix_two
    z_two = nn_dot(w2t[...], mix_two)
    dz_two = (cot_ref[...].astype(F32) * slope_of(z_two)).astype(BF16)
    spread(1, nn_dot(w2[...], dz_two).astype(BF16), i, dmb.at[0], dmr.at[0], False)
    g2_ref[...] = nt_dot(mix[1], dz_two)
    transposed(0)
    dh_one = gathered(2)
    dz_one = (dh_one.astype(F32) * slope_of(z1[...])).astype(BF16)
    spread(2, nn_dot(w1[...], dz_one).astype(BF16), i, dmb.at[1], dmr.at[1], False)
    g1_ref[...] = nt_dot(mix[0], dz_one)
    transposed(1)
    for a in range(R):
        for q in range(F):
            done(fin.at[a, q], xr.at[3, a, q])
    for q in range(F):
        total = fin[0, q].astype(F32)
        for a in range(1, R):
            total = total + fin[a, q].astype(F32)
        out_ref[:, q * C:(q + 1) * C] = total.astype(BF16)

    one = pst.at[0, 0]

    @pl.when(r != 0)
    def _():
        for q in range(F):
            done(one, p0s.at[q])

    for p in range(2):
        def sent_chunk(n, carry):
            s, q = lax.div(n, F), lax.rem(n, F)

            @pl.when((s < H - 1) | (q < half))
            def _():
                done(one, fs.at[p, s, q])

            @pl.when((s < H - 1) | (q >= half))
            def _():
                done(one, bs.at[p, s, q])

            @pl.when((s > 0) | (q < half))
            def _():
                done(one, ds.at[p, s, q])

            @pl.when((s > 0) | (q >= half))
            def _():
                done(one, us.at[p, s, q])

            return carry

        lax.fori_loop(0, H * F, sent_chunk, 0)
    for a in range(R):
        for b in range(F):
            if (a, b) != (0, 0):
                done(one, xs.at[0, a, b])
                done(one, xs.at[1, a, b])
            if a:
                done(one, xs.at[2, a, b])
                done(one, xs.at[3, a, b])

    for b in range(F):
        pl.when(jnp.logical_not((r == 0) & (f == b)))(functools.partial(done, one, xs.at[2, 0, b]))
        pl.when(r != 0)(functools.partial(done, one, xs.at[3, 0, b]))
        pl.when(jnp.logical_not((r == 0) & (f == b)))(functools.partial(done, one, ls.at[0, b]))
        pl.when(f != b)(functools.partial(done, one, ls.at[1, b]))
        pl.when(f != b)(functools.partial(done, one, ls.at[2, b]))


def shards(features, tile_values, tile_coords, section_counts, weight_one, weight_two, cotangent):
    L, R, F = (lax.axis_size(n) for n in ("loop", "rep", "feat"))
    S = L // R
    H = S // 2
    tile_set = tile_values[0, 0]
    d, nodes = features.shape
    D = weight_one.shape[0]
    C = nodes // F
    filled = section_counts[0, 0]
    slots = tile_set.shape[0]
    ends = jnp.cumsum(filled)
    starts = jnp.minimum(ends - filled, slots)
    ends = jnp.minimum(ends, slots)
    dense = dense_sections(tile_set, tile_coords[0, 0, 0], tile_coords[0, 0, 1], starts, ends, F, nodes)
    scale = 1.0 / math.sqrt(nodes * L)
    vmem = pl.BlockSpec(memory_space=pltpu.VMEM)
    dma = pltpu.SemaphoreType.DMA
    input_grad, g1, g2 = pl.pallas_call(
        functools.partial(layers_kernel, (L, R, F)),
        out_shape=(
            jax.ShapeDtypeStruct((d, nodes), BF16),
            jax.ShapeDtypeStruct((D, D), F32),
            jax.ShapeDtypeStruct((D, D), F32),
        ),
        in_specs=[vmem, pl.BlockSpec(memory_space=pl.ANY)] + [vmem] * 5,
        out_specs=(vmem,) * 3,
        scratch_shapes=[
            pltpu.VMEM((S, F, nodes, C), BF16),
            pltpu.VMEM((2, S, F, d, C), BF16),
            pltpu.VMEM((d, nodes), F32),
            pltpu.VMEM((4, F, d, C), BF16),
            pltpu.VMEM((3, R, F, d, C), BF16),
            pltpu.VMEM((R, F, d, C), BF16),
            pltpu.VMEM((3, F, d, C), BF16),
            pltpu.VMEM((2, F, d, C), BF16),
            pltpu.VMEM((d, nodes), BF16),
            pltpu.VMEM((D, C), F32),
            pltpu.VMEM((2, D, C), BF16),
        ]
        + [pltpu.VMEM((2, H, F, d, C), BF16)] * 4
        + [
            dma((S,)), dma((2, S, F)), dma((2, H, F)), dma((2, H, F)),
            dma((4, R, F)), dma((4, R, F)), dma((3, F)), dma((2, F)), dma((F,)),
            dma((2, H, F)), dma((2, H, F)), dma((2, H, F)), dma((2, H, F)),
        ],
        compiler_params=pltpu.CompilerParams(
            collective_id=0, has_side_effects=True, vmem_limit_bytes=48 * 1024 * 1024
        ),
        name="layers",
    )(features, dense, weight_one, weight_one.T, weight_two, weight_two.T, cotangent)
    g1, g2 = lax.psum((g1 * scale, g2 * scale), ("loop", "feat"))
    return (g1, g2, input_grad)


def solution(mesh):
    return jax.shard_map(
        shards,
        mesh=mesh,
        in_specs=(
            P("feat", "loop"),
            P("loop", "rep", None, None, None),
            P("loop", "rep", None, None),
            P("loop", "rep", None),
            P(),
            P(),
            P(None, ("loop", "feat")),
        ),
        out_specs=(P(), P(), P("feat", "loop")),
        check_vma=False,
    )
```

```python
import functools
import math

import jax
import jax.numpy as jnp
from jax import lax
from jax.experimental import pallas as pl
from jax.experimental.pallas import tpu as pltpu
from jax.sharding import PartitionSpec as P

MESH = pl.DeviceIdType.MESH
BF16 = jnp.bfloat16
F32 = jnp.float32


def place_kernel(coords, counts, tiles_hbm, out, tiles, sem):
    copy = pltpu.make_async_copy(tiles_hbm.at[0, 0], tiles, sem)
    copy.start()
    slots, side = tiles.shape[:2]
    sections = out.shape[0]
    per_chunk = out.shape[-1] // side

    def clear(n, carry):
        out[n] = jnp.zeros(out.shape[1:], out.dtype)
        return carry

    lax.fori_loop(0, sections, clear, 0)
    copy.wait()

    def one_section(section, start):
        end = jnp.minimum(start + counts[0, 0, section], slots)

        def one_tile(slot, carry):
            row = pl.multiple_of(coords[0, 0, 0, slot] * side, side)
            col = coords[0, 0, 1, slot]
            lane = pl.multiple_of(lax.rem(col, per_chunk) * side, side)
            out[section, lax.div(col, per_chunk), pl.ds(row, side), pl.ds(lane, side)] = tiles[slot]
            return carry

        lax.fori_loop(start, end, one_tile, 0)
        return end

    lax.fori_loop(0, sections, one_section, 0)


def dense_sections(tile_values, tile_coords, section_counts, chunks, nodes):
    sections = section_counts.shape[-1]
    smem = pl.BlockSpec(memory_space=pltpu.SMEM)
    return pl.pallas_call(
        place_kernel,
        out_shape=jax.ShapeDtypeStruct((sections, chunks, nodes, nodes // chunks), BF16),
        in_specs=[smem, smem, pl.BlockSpec(memory_space=pltpu.HBM)],
        out_specs=pl.BlockSpec(memory_space=pltpu.VMEM),
        scratch_shapes=[pltpu.VMEM(tile_values.shape[2:], BF16), pltpu.SemaphoreType.DMA],
        compiler_params=pltpu.CompilerParams(vmem_limit_bytes=8 * 1024 * 1024),
        name="place_tiles",
    )(tile_coords, section_counts, tile_values)


def nt_dot(a, b):
    return lax.dot_general(a, b, (((1,), (1,)), ((), ())), preferred_element_type=F32)


def nn_dot(a, b):
    return lax.dot_general(a, b, (((1,), (0,)), ((), ())), preferred_element_type=F32)


def slope_of(z):
    s = 1.0 / (1.0 + jnp.exp(-z))
    return s * (1.0 + z * (1.0 - s))


def layers_kernel(
    sizes, scale,
    feat_ref, dense, w1, w2, cot_ref,
    out_ref, g1_ref, g2_ref,
    hbuf, acc, pst, ebuf, fin, lst, dmb, dmf, z1, mix, rd, ru, sd, su, wt, gst, gin, gring, gsum, gall,
    gss, gsr, gus, gds, grr, gas, gar, ringr, fs, bs, xs, xr, ls, dmr, p0s, rdr, rur, ds, us,
):
    L, R, F = sizes
    S = L // R
    H = S // 2
    half = F // 2
    C = hbuf.shape[-1]
    i, r, f = lax.axis_index("loop"), lax.axis_index("rep"), lax.axis_index("feat")

    def at_loop(value):
        return lax.rem(value + L, L)

    up, dn = at_loop(i + R), at_loop(i - R)
    ahead, behind = at_loop(i + r), at_loop(i - r)
    block, me = lax.div(i, R), lax.rem(i, R)
    first_of_block = block * R

    def local(src, dst, sem):
        return pltpu.make_async_copy(src, dst, sem)

    def remote(src, dst, ssem, rsem, to):
        return pltpu.make_async_remote_copy(
            src_ref=src, dst_ref=dst, send_sem=ssem, recv_sem=rsem,
            device_id=to, device_id_type=MESH,
        )

    def done(ref, sem):
        pltpu.make_async_copy(ref, ref, sem).wait()

    barrier = pltpu.get_barrier_semaphore()

    def greet(*to):
        pl.semaphore_signal(barrier, inc=1, device_id=to, device_id_type=MESH)

    greet(up, r, f)
    greet(dn, r, f)
    for a in range(R):
        for b in range(F):
            if (a, b) != (0, 0):
                greet(i, lax.rem(r + a, R), lax.rem(f + b, F))

    @pl.when(r != 0)
    def _():
        for b in range(F):
            greet(behind, r, b)

    for a in range(1, R):
        for b in range(F):
            greet(at_loop(i + a), a, b)
    for a in range(1, R):
        for b in range(F):
            greet(first_of_block + lax.rem(me + a, R), r, b)
    zero = jnp.zeros(rd.shape[3:], BF16)
    for p in range(2):
        for q in range(F):
            if q >= half:
                rd[p, 0, q] = zero
            else:
                ru[p, 0, q] = zero
    wt[0] = w1[...].T
    wt[1] = w2[...].T
    pl.semaphore_wait(barrier, 1 + R * F + (R - 1) * F + jnp.where(r != 0, F + R * F, 0))

    for q in range(F):
        src = feat_ref.at[:, pl.ds(q * C, C)]

        @pl.when(r == 0)
        def _():
            local(src, hbuf.at[0, 0, q], ringr.at[0, 0, q]).start()

        @pl.when(r != 0)
        def _():
            remote(src, hbuf.at[0, 0, q], p0s.at[q], ringr.at[0, 0, q], (ahead, r, f)).start()

    def forward(p):
        def send_up(k, q):
            return remote(hbuf.at[p, k, q], hbuf.at[p, k + 1, q], fs.at[p, k, q], ringr.at[p, k + 1, q], (up, r, f))

        def send_dn(k, s, q):
            to = S - 1 - s
            return remote(hbuf.at[p, k, q], hbuf.at[p, to, q], bs.at[p, s, q], ringr.at[p, to, q], (dn, r, f))

        def term(k, q):
            return nt_dot(hbuf[p, k, q], dense[k, q])

        def first(q, carry):
            done(hbuf.at[p, 0, q], ringr.at[p, 0, q])
            send_up(0, q).start()
            send_dn(0, 0, q).start()

            @pl.when(q == 0)
            def _():
                acc[...] = term(0, q)

            @pl.when(q != 0)
            def _():
                acc[...] += term(0, q)

            return carry

        lax.fori_loop(0, F, first, 0)

        def stage(s, carry):
            kb = S - s
            def chunk(q, inner):
                done(hbuf.at[p, s, q], ringr.at[p, s, q])

                @pl.when((s < H - 1) | (q < half))
                def _():
                    send_up(s, q).start()

                done(hbuf.at[p, kb, q], ringr.at[p, kb, q])

                @pl.when((s < H - 1) | (q >= half))
                def _():
                    send_dn(kb, s, q).start()

                acc[...] += term(s, q) + term(kb, q)
                return inner

            return lax.fori_loop(0, F, chunk, carry)

        lax.fori_loop(1, H, stage, 0)
        def last(q, carry):
            done(hbuf.at[p, H, q], ringr.at[p, H, q])
            acc[...] += term(H, q)
            return carry

        lax.fori_loop(0, F, last, 0)
        for q in range(F):
            pst[p, q] = acc[:, q * C:(q + 1) * C].astype(BF16)
        for a in range(R):
            for b in range(F):
                rr, q = lax.rem(r + a, R), lax.rem(f + b, F)
                if (a, b) == (0, 0):
                    local(pst.at[p, q], ebuf.at[p, r, f], xr.at[p, r, f]).start()
                else:
                    remote(pst.at[p, q], ebuf.at[p, r, f], xs.at[p, a, b], xr.at[p, r, f], (i, rr, q)).start()

    def gathered(e):
        total = None
        for a in range(R):
            for b in range(F):
                done(ebuf.at[e, a, b], xr.at[e, a, b])
        for a in range(R):
            part = ebuf[e, a].reshape(z1.shape).astype(F32)
            total = part if total is None else total + part
        return total.astype(BF16)

    def spread(n, value, to_loop, dst, sem, shifted):
        lst[n] = value.reshape(lst.shape[1:])
        for b in range(F):
            ff = lax.rem(f + b, F)

            def away():
                remote(lst.at[n, ff], dst.at[f], ls.at[n, ff], sem.at[f], (to_loop, r, ff)).start()

            def here():
                local(lst.at[n, ff], dst.at[f], sem.at[f]).start()

            if b:
                away()
            elif shifted:
                pl.when(r == 0)(here)
                pl.when(r != 0)(away)
            else:
                here()

    def grad_start(g, value):
        gst[g] = value.reshape(gst.shape[1:])
        for a in range(R):
            for b in range(F):
                c, ff = lax.rem(me + a, R), lax.rem(f + b, F)
                if (a, b) == (0, 0):
                    local(gst.at[g, r, f], gin.at[g, me, f], gsr.at[g, me, f]).start()
                else:
                    to = (first_of_block + c, r, ff)
                    remote(gst.at[g, r, ff], gin.at[g, me, f], gss.at[g, a, b], gsr.at[g, me, f], to).start()

    def grad_up(g, s):
        slot = lax.rem(block + S - s, S)
        return remote(gring.at[g, slot], gring.at[g, slot], gus.at[g, s], grr.at[g, slot], (up, r, f))

    def grad_dn(g, s):
        slot = lax.rem(block + s, S)
        return remote(gring.at[g, slot], gring.at[g, slot], gds.at[g, s], grr.at[g, slot], (dn, r, f))

    def grad_block(g):
        total = None
        for a in range(R):
            for b in range(F):
                done(gin.at[g, a, b], gsr.at[g, a, b])
        for a in range(R):
            for b in range(F):
                total = gin[g, a, b] if total is None else total + gin[g, a, b]
        gring[g, block] = total
        grad_up(g, 0).start()
        grad_dn(g, 0).start()

    def grad_hop(g, s):
        below, above = lax.rem(block + S - s, S), lax.rem(block + s, S)
        done(gring.at[g, below], grr.at[g, below])
        grad_up(g, s).start()
        done(gring.at[g, above], grr.at[g, above])

        @pl.when(s < H - 1)
        def _():
            grad_dn(g, s).start()

    def grad_spread(g):
        far = lax.rem(block + H, S)
        done(gring.at[g, far], grr.at[g, far])
        total = gring[g, 0]
        for n in range(1, S):
            total = total + gring[g, n]
        gsum[g] = total * scale
        for a in range(R):
            for b in range(F):
                if (a, b) == (0, 0):
                    local(gsum.at[g], gall.at[g, r, f], gar.at[g, r, f]).start()
                else:
                    to = (i, lax.rem(r + a, R), lax.rem(f + b, F))
                    remote(gsum.at[g], gall.at[g, r, f], gas.at[g, a, b], gar.at[g, r, f], to).start()

    def grad_end(g, ref):
        for a in range(R):
            for b in range(F):
                done(gall.at[g, a, b], gar.at[g, a, b])
        ref[...] = gall[g].reshape(ref.shape)

    def transposed(p):
        for q in range(F):
            done(dmb.at[p, q], dmr.at[p, q])
            dmf[:, q * C:(q + 1) * C] = dmb[p, q]

        def send_dn(s, q):
            return remote(sd.at[p, s, q], rd.at[p, s, q], ds.at[p, s, q], rdr.at[p, s, q], (dn, r, f))

        def send_up(s, q):
            return remote(su.at[p, s, q], ru.at[p, s, q], us.at[p, s, q], rur.at[p, s, q], (up, r, f))

        def first(q, carry):
            value = nn_dot(dmf[...], dense[H, q]).astype(BF16)

            @pl.when(q < half)
            def _():
                sd[p, 0, q] = value
                send_dn(0, q).start()

            @pl.when(q >= half)
            def _():
                su[p, 0, q] = value
                send_up(0, q).start()

            return carry

        lax.fori_loop(0, F, first, 0)
        grad_block(p)

        def stage(s, carry):
            def chunk(q, inner):
                down = nn_dot(dmf[...], dense[H - s, q])
                above = nn_dot(dmf[...], dense[H + s, q])

                @pl.when((s > 1) | (q < half))
                def _():
                    done(rd.at[p, s - 1, q], rdr.at[p, s - 1, q])

                sd[p, s, q] = (down + rd[p, s - 1, q].astype(F32)).astype(BF16)
                send_dn(s, q).start()

                @pl.when((s > 1) | (q >= half))
                def _():
                    done(ru.at[p, s - 1, q], rur.at[p, s - 1, q])

                su[p, s, q] = (above + ru[p, s - 1, q].astype(F32)).astype(BF16)
                send_up(s, q).start()
                return inner

            lax.fori_loop(0, F, chunk, carry)
            grad_hop(p, s)
            return carry

        lax.fori_loop(1, H, stage, 0)
        x = 2 + p

        def last(q, carry):
            own = nn_dot(dmf[...], dense[0, q])
            done(rd.at[p, H - 1, q], rdr.at[p, H - 1, q])
            done(ru.at[p, H - 1, q], rur.at[p, H - 1, q])
            own = own + rd[p, H - 1, q].astype(F32) + ru[p, H - 1, q].astype(F32)
            pst[x, q] = own.astype(BF16)
            for a in range(R):
                rr = lax.rem(r + a, R)
                if p == 0:
                    dst, sem, to, mine = ebuf.at[2, r, f], xr.at[2, r, f], (behind, rr, q), (r == 0) & (q == f)
                else:
                    dst, sem, to, mine = fin.at[r, q], xr.at[3, r, q], (behind, rr, f), r == 0

                def away():
                    remote(pst.at[x, q], dst, xs.at[x, a, q], sem, to).start()

                if a:
                    away()
                else:
                    pl.when(mine)(lambda: local(pst.at[x, q], dst, sem).start())
                    pl.when(jnp.logical_not(mine))(away)
            return carry

        lax.fori_loop(0, F, last, 0)
        grad_spread(p)

    forward(0)
    mix_one = gathered(0)
    mix[0] = mix_one
    z_one = nn_dot(wt[0], mix_one)
    z1[...] = z_one
    h_one = (z_one / (1.0 + jnp.exp(-z_one))).astype(BF16)
    spread(0, h_one, ahead, hbuf.at[1, 0], ringr.at[1, 0], True)
    forward(1)
    mix_two = gathered(1)
    mix[1] = mix_two
    z_two = nn_dot(wt[1], mix_two)
    dz_two = (cot_ref[...].astype(F32) * slope_of(z_two)).astype(BF16)
    spread(1, nn_dot(w2[...], dz_two).astype(BF16), i, dmb.at[0], dmr.at[0], False)
    grad_start(0, nt_dot(mix[1], dz_two))
    transposed(0)
    dh_one = gathered(2)
    dz_one = (dh_one.astype(F32) * slope_of(z1[...])).astype(BF16)
    spread(2, nn_dot(w1[...], dz_one).astype(BF16), i, dmb.at[1], dmr.at[1], False)
    grad_start(1, nt_dot(mix[0], dz_one))
    transposed(1)
    for a in range(R):
        for q in range(F):
            done(fin.at[a, q], xr.at[3, a, q])
    for q in range(F):
        total = fin[0, q].astype(F32)
        for a in range(1, R):
            total = total + fin[a, q].astype(F32)
        out_ref[:, q * C:(q + 1) * C] = total.astype(BF16)

    grad_end(0, g2_ref)
    grad_end(1, g1_ref)

    one = pst.at[0, 0]

    @pl.when(r != 0)
    def _():
        for q in range(F):
            done(one, p0s.at[q])

    for p in range(2):
        def sent_chunk(n, carry):
            s, q = lax.div(n, F), lax.rem(n, F)

            @pl.when((s < H - 1) | (q < half))
            def _():
                done(one, fs.at[p, s, q])

            @pl.when((s < H - 1) | (q >= half))
            def _():
                done(one, bs.at[p, s, q])

            @pl.when((s > 0) | (q < half))
            def _():
                done(one, ds.at[p, s, q])

            @pl.when((s > 0) | (q >= half))
            def _():
                done(one, us.at[p, s, q])

            return carry

        lax.fori_loop(0, H * F, sent_chunk, 0)
        piece = gsum.at[0]
        for s in range(H):
            done(piece, gus.at[p, s])
            if s < H - 1:
                done(piece, gds.at[p, s])
        for a in range(R):
            for b in range(F):
                if (a, b) != (0, 0):
                    done(piece, gss.at[p, a, b])
                    done(piece, gas.at[p, a, b])
    for a in range(R):
        for b in range(F):
            if (a, b) != (0, 0):
                done(one, xs.at[0, a, b])
                done(one, xs.at[1, a, b])
            if a:
                done(one, xs.at[2, a, b])
                done(one, xs.at[3, a, b])

    for b in range(F):
        pl.when(jnp.logical_not((r == 0) & (f == b)))(functools.partial(done, one, xs.at[2, 0, b]))
        pl.when(r != 0)(functools.partial(done, one, xs.at[3, 0, b]))
        pl.when(jnp.logical_not((r == 0) & (f == b)))(functools.partial(done, one, ls.at[0, b]))
        pl.when(f != b)(functools.partial(done, one, ls.at[1, b]))
        pl.when(f != b)(functools.partial(done, one, ls.at[2, b]))


def shards(features, tile_values, tile_coords, section_counts, weight_one, weight_two, cotangent):
    L, R, F = (lax.axis_size(n) for n in ("loop", "rep", "feat"))
    S = L // R
    H = S // 2
    d, nodes = features.shape
    D = weight_one.shape[0]
    C = nodes // F
    piece = D // (R * F)
    dense = dense_sections(tile_values, tile_coords, section_counts, F, nodes)
    scale = 1.0 / math.sqrt(nodes * L)
    vmem = pl.BlockSpec(memory_space=pltpu.VMEM)
    dma = pltpu.SemaphoreType.DMA
    input_grad, g1, g2 = pl.pallas_call(
        functools.partial(layers_kernel, (L, R, F), scale),
        out_shape=(
            jax.ShapeDtypeStruct((d, nodes), BF16),
            jax.ShapeDtypeStruct((D, D), F32),
            jax.ShapeDtypeStruct((D, D), F32),
        ),
        in_specs=[vmem] * 5,
        out_specs=(vmem,) * 3,
        scratch_shapes=[
            pltpu.VMEM((2, S, F, d, C), BF16),
            pltpu.VMEM((d, nodes), F32),
            pltpu.VMEM((4, F, d, C), BF16),
            pltpu.VMEM((3, R, F, d, C), BF16),
            pltpu.VMEM((R, F, d, C), BF16),
            pltpu.VMEM((3, F, d, C), BF16),
            pltpu.VMEM((2, F, d, C), BF16),
            pltpu.VMEM((d, nodes), BF16),
            pltpu.VMEM((D, C), F32),
            pltpu.VMEM((2, D, C), BF16),
        ]
        + [pltpu.VMEM((2, H, F, d, C), BF16)] * 4
        + [
            pltpu.VMEM((2, D, D), BF16),
            pltpu.VMEM((2, R, F, piece, D), F32),
            pltpu.VMEM((2, R, F, piece, D), F32),
            pltpu.VMEM((2, S, piece, D), F32),
            pltpu.VMEM((2, piece, D), F32),
            pltpu.VMEM((2, R, F, piece, D), F32),
            dma((2, R, F)), dma((2, R, F)), dma((2, H)), dma((2, H)), dma((2, S)), dma((2, R, F)), dma((2, R, F)),
            dma((2, S, F)), dma((2, H, F)), dma((2, H, F)),
            dma((4, R, F)), dma((4, R, F)), dma((3, F)), dma((2, F)), dma((F,)),
            dma((2, H, F)), dma((2, H, F)), dma((2, H, F)), dma((2, H, F)),
        ],
        compiler_params=pltpu.CompilerParams(
            collective_id=0, has_side_effects=True, vmem_limit_bytes=24 * 1024 * 1024
        ),
        name="layers",
    )(features, dense, weight_one, weight_two, cotangent)
    return (g1, g2, input_grad)


def solution(mesh):
    return jax.shard_map(
        shards,
        mesh=mesh,
        in_specs=(
            P("feat", "loop"),
            P("loop", "rep", None, None, None),
            P("loop", "rep", None, None),
            P("loop", "rep", None),
            P(),
            P(),
            P(None, ("loop", "feat")),
        ),
        out_specs=(P(), P(), P("feat", "loop")),
        check_vma=False,
    )
```

```python
import functools
import math

import jax
import jax.numpy as jnp
from jax import lax
from jax.experimental import pallas as pl
from jax.experimental.pallas import tpu as pltpu
from jax.sharding import PartitionSpec as P

MESH = pl.DeviceIdType.MESH
BF16 = jnp.bfloat16
F32 = jnp.float32


def place_kernel(coords_hbm, counts_hbm, tiles_hbm, out, coords, counts, tiles, sems):
    pairs = ((coords_hbm, coords), (counts_hbm, counts), (tiles_hbm.at[0, 0], tiles))
    copies = [pltpu.make_async_copy(src, dst, sems.at[n]) for n, (src, dst) in enumerate(pairs)]
    for copy in copies:
        copy.start()
    slots, side = tiles.shape[:2]
    sections = out.shape[0]
    per_chunk = out.shape[-1] // side

    def clear(n, carry):
        out[n] = jnp.zeros(out.shape[1:], out.dtype)
        return carry

    lax.fori_loop(0, sections, clear, 0)
    for copy in copies:
        copy.wait()

    def one_section(section, start):
        end = jnp.minimum(start + counts[0, 0, section], slots)

        def one_tile(slot, carry):
            row = pl.multiple_of(coords[0, 0, 0, slot] * side, side)
            col = coords[0, 0, 1, slot]
            lane = pl.multiple_of(lax.rem(col, per_chunk) * side, side)
            out[section, lax.div(col, per_chunk), pl.ds(row, side), pl.ds(lane, side)] = tiles[slot]
            return carry

        lax.fori_loop(start, end, one_tile, 0)
        return end

    lax.fori_loop(0, sections, one_section, 0)


def dense_sections(tile_values, tile_coords, section_counts, chunks, nodes):
    sections = section_counts.shape[-1]
    hbm = pl.BlockSpec(memory_space=pltpu.HBM)
    return pl.pallas_call(
        place_kernel,
        out_shape=jax.ShapeDtypeStruct((sections, chunks, nodes, nodes // chunks), BF16),
        in_specs=[hbm] * 3,
        out_specs=pl.BlockSpec(memory_space=pltpu.VMEM),
        scratch_shapes=[
            pltpu.SMEM(tile_coords.shape, jnp.int32),
            pltpu.SMEM(section_counts.shape, jnp.int32),
            pltpu.VMEM(tile_values.shape[2:], BF16),
            pltpu.SemaphoreType.DMA((3,)),
        ],
        compiler_params=pltpu.CompilerParams(vmem_limit_bytes=8 * 1024 * 1024),
        name="place_tiles",
    )(*(pltpu.with_memory_space_constraint(a, pltpu.HBM) for a in (tile_coords, section_counts, tile_values)))


def nt_dot(a, b):
    return lax.dot_general(a, b, (((1,), (1,)), ((), ())), preferred_element_type=F32)


def nn_dot(a, b):
    return lax.dot_general(a, b, (((1,), (0,)), ((), ())), preferred_element_type=F32)


def slope_of(z):
    s = 1.0 / (1.0 + jnp.exp(-z))
    return s * (1.0 + z * (1.0 - s))


def layers_kernel(
    sizes, scale,
    feat_ref, dense, w1, w2, cot_ref,
    out_ref, g1_ref, g2_ref,
    hbuf, acc, pst, ebuf, fin, lst, dmb, dmf, z1, mix, rd, ru, sd, su, wt, gst, gin, gring, gsum, gall,
    gss, gsr, gus, grr, gas, gar, ringr, fs, bs, xs, xr, ls, dmr, p0s, h0s, rdr, rur, ds, us,
):
    L, R, F = sizes
    S = L // R
    H = S // 2
    half = F // 2
    far_first = sorted(range(R), key=lambda a: -min(a, R - a))
    C = hbuf.shape[-1]
    i, r, f = lax.axis_index("loop"), lax.axis_index("rep"), lax.axis_index("feat")

    def at_loop(value):
        return lax.rem(value + 2 * L, L)

    up, dn = at_loop(i + R), at_loop(i - R)
    up2, dn2 = at_loop(i + 2 * R), at_loop(i - 2 * R)
    ahead, behind = at_loop(i + r), at_loop(i - r)
    block, me = lax.div(i, R), lax.rem(i, R)
    first_of_block = block * R

    def local(src, dst, sem):
        return pltpu.make_async_copy(src, dst, sem)

    def remote(src, dst, ssem, rsem, to):
        return pltpu.make_async_remote_copy(
            src_ref=src, dst_ref=dst, send_sem=ssem, recv_sem=rsem,
            device_id=to, device_id_type=MESH,
        )

    def done(ref, sem):
        pltpu.make_async_copy(ref, ref, sem).wait()

    barrier = pltpu.get_barrier_semaphore()

    def greet(*to):
        pl.semaphore_signal(barrier, inc=1, device_id=to, device_id_type=MESH)

    for m in range(1, S):
        greet(at_loop(i + m * R), r, f)
    for b in range(F):
        greet(at_loop(behind - R), r, b)
        greet(at_loop(behind + R), r, b)
    for a in range(R):
        for b in range(F):
            if (a, b) != (0, 0):
                greet(i, lax.rem(r + a, R), lax.rem(f + b, F))

    @pl.when(r != 0)
    def _():
        for b in range(F):
            greet(behind, r, b)

    for a in range(1, R):
        for b in range(F):
            greet(at_loop(i + a), a, b)
    for a in range(1, R):
        for b in range(F):
            greet(first_of_block + lax.rem(me + a, R), r, b)
    zero = jnp.zeros(rd.shape[3:], BF16)
    for p in range(2):
        for q in range(F):
            if q >= half:
                rd[p, 1, q] = zero
            else:
                ru[p, 1, q] = zero
    wt[0] = w1[...].T
    wt[1] = w2[...].T
    pl.semaphore_wait(barrier, S - 1 + 2 * F + R * F - 1 + (R - 1) * F + jnp.where(r != 0, F + R * F, 0))

    def to_ring(p, src, q, ssem, ff):
        for n, (k, to) in enumerate(((1, at_loop(ahead + R)), (S - 1, at_loop(ahead - R)), (0, ahead))):
            def away(n=n, k=k, to=to):
                remote(src, hbuf.at[p, k, q], ssem.at[n], ringr.at[p, k, q], (to, r, ff)).start()

            def here(k=k):
                local(src, hbuf.at[p, k, q], ringr.at[p, k, q]).start()

            if k:
                away()
            else:
                mine = (r == 0) & (ff == f)
                pl.when(mine)(here)
                pl.when(jnp.logical_not(mine))(away)

    for q in range(F):
        to_ring(0, feat_ref.at[:, pl.ds(q * C, C)], q, p0s.at[q], f)

    def forward(p):
        def hop(k, to_k, q, ssem, to):
            remote(hbuf.at[p, k, q], hbuf.at[p, to_k, q], ssem, ringr.at[p, to_k, q], (to, r, f)).start()

        def here(k, q):
            done(hbuf.at[p, k, q], ringr.at[p, k, q])

        def term(k, q):
            return nt_dot(hbuf[p, k, q], dense[k, q])

        def near(q, carry):
            here(1, q)
            hop(1, 2, q, fs.at[p, 0, q], up)
            here(S - 1, q)
            hop(S - 1, S - 2, q, bs.at[p, 0, q], dn)
            here(0, q)
            value = term(0, q) + term(1, q) + term(S - 1, q)

            @pl.when(q == 0)
            def _():
                acc[...] = value

            @pl.when(q != 0)
            def _():
                acc[...] += value

            return carry

        lax.fori_loop(0, F, near, 0)

        def middle(q, carry):
            here(2, q)

            @pl.when(q < half)
            def _():
                hop(2, H, q, fs.at[p, 2, q], up2)

            hop(2, 3, q, fs.at[p, 1, q], up)
            here(S - 2, q)

            @pl.when(q >= half)
            def _():
                hop(S - 2, H, q, bs.at[p, 2, q], dn2)

            hop(S - 2, S - 3, q, bs.at[p, 1, q], dn)
            acc[...] += term(2, q) + term(S - 2, q)
            return carry

        lax.fori_loop(0, F, middle, 0)

        def far(q, carry):
            here(3, q)
            here(S - 3, q)
            here(H, q)
            acc[...] += term(3, q) + term(S - 3, q) + term(H, q)
            return carry

        lax.fori_loop(0, F, far, 0)
        for q in range(F):
            pst[p, q] = acc[:, q * C:(q + 1) * C].astype(BF16)
        for a in far_first:
            for b in range(F):
                rr, q = lax.rem(r + a, R), lax.rem(f + b, F)
                if (a, b) == (0, 0):
                    local(pst.at[p, q], ebuf.at[p, r, f], xr.at[p, r, f]).start()
                else:
                    remote(pst.at[p, q], ebuf.at[p, r, f], xs.at[p, a, b], xr.at[p, r, f], (i, rr, q)).start()

    def gathered(e):
        total = None
        for a in range(R):
            for b in range(F):
                done(ebuf.at[e, a, b], xr.at[e, a, b])
        for a in range(R):
            part = ebuf[e, a].reshape(z1.shape).astype(F32)
            total = part if total is None else total + part
        return total.astype(BF16)

    def spread(n, value, dst, sem):
        lst[n] = value.reshape(lst.shape[1:])
        for b in range(F):
            ff = lax.rem(f + b, F)
            if n == 0:
                to_ring(1, lst.at[n, ff], f, h0s.at[ff], ff)
            elif b:
                remote(lst.at[n, ff], dst.at[f], ls.at[n, ff], sem.at[f], (i, r, ff)).start()
            else:
                local(lst.at[n, ff], dst.at[f], sem.at[f]).start()

    def grad_start(g, value):
        gst[g] = value.reshape(gst.shape[1:])
        for a in range(R):
            for b in range(F):
                c, ff = lax.rem(me + a, R), lax.rem(f + b, F)
                if (a, b) == (0, 0):
                    local(gst.at[g, r, f], gin.at[g, me, f], gsr.at[g, me, f]).start()
                else:
                    to = (first_of_block + c, r, ff)
                    remote(gst.at[g, r, ff], gin.at[g, me, f], gss.at[g, a, b], gsr.at[g, me, f], to).start()

    def grad_send(g, m):
        slot = gring.at[g, block]
        return remote(slot, slot, gus.at[g, m], grr.at[g, block], (at_loop(i + m * R), r, f))

    def grad_block(g):
        total = None
        for a in range(R):
            for b in range(F):
                done(gin.at[g, a, b], gsr.at[g, a, b])
        for a in range(R):
            for b in range(F):
                total = gin[g, a, b] if total is None else total + gin[g, a, b]
        gring[g, block] = total
        for m in range(1, S):
            grad_send(g, m).start()

    def grad_spread(g):
        for m in range(1, S):
            other = lax.rem(block + m, S)
            done(gring.at[g, other], grr.at[g, other])
        total = gring[g, 0]
        for n in range(1, S):
            total = total + gring[g, n]
        gsum[g] = total * scale
        for a in range(R):
            for b in range(F):
                if (a, b) == (0, 0):
                    local(gsum.at[g], gall.at[g, r, f], gar.at[g, r, f]).start()
                else:
                    to = (i, lax.rem(r + a, R), lax.rem(f + b, F))
                    remote(gsum.at[g], gall.at[g, r, f], gas.at[g, a, b], gar.at[g, r, f], to).start()

    def grad_end(g, ref):
        for a in range(R):
            for b in range(F):
                done(gall.at[g, a, b], gar.at[g, a, b])
        ref[...] = gall[g].reshape(ref.shape)

    def transposed(p):
        for q in range(F):
            done(dmb.at[p, q], dmr.at[p, q])
            dmf[:, q * C:(q + 1) * C] = dmb[p, q]

        def send_dn(s, q, to=dn):
            remote(sd.at[p, s, q], rd.at[p, s, q], ds.at[p, s, q], rdr.at[p, s, q], (to, r, f)).start()

        def send_up(s, q, to=up):
            remote(su.at[p, s, q], ru.at[p, s, q], us.at[p, s, q], rur.at[p, s, q], (to, r, f)).start()

        def term(k, q):
            return nn_dot(dmf[...], dense[k, q])

        def from_dn(s, q):
            done(rd.at[p, s, q], rdr.at[p, s, q])

        def from_up(s, q):
            done(ru.at[p, s, q], rur.at[p, s, q])

        def far(q, carry):
            value = term(H, q).astype(BF16)

            @pl.when(q < half)
            def _():
                sd[p, 1, q] = value
                send_dn(1, q, dn2)

            @pl.when(q >= half)
            def _():
                su[p, 1, q] = value
                send_up(1, q, up2)

            sd[p, 0, q] = term(3, q).astype(BF16)
            send_dn(0, q)
            su[p, 0, q] = term(S - 3, q).astype(BF16)
            send_up(0, q)
            return carry

        lax.fori_loop(0, F, far, 0)

        def middle(q, carry):
            down, above = term(2, q), term(S - 2, q)
            from_dn(0, q)
            pl.when(q < half)(lambda: from_dn(1, q))
            sd[p, 2, q] = (down + rd[p, 0, q].astype(F32) + rd[p, 1, q].astype(F32)).astype(BF16)
            send_dn(2, q)
            from_up(0, q)
            pl.when(q >= half)(lambda: from_up(1, q))
            su[p, 2, q] = (above + ru[p, 0, q].astype(F32) + ru[p, 1, q].astype(F32)).astype(BF16)
            send_up(2, q)
            return carry

        lax.fori_loop(0, F, middle, 0)
        grad_block(p)

        def near(q, carry):
            down, above = term(1, q), term(S - 1, q)
            from_dn(2, q)
            sd[p, 3, q] = (down + rd[p, 2, q].astype(F32)).astype(BF16)
            send_dn(3, q)
            from_up(2, q)
            su[p, 3, q] = (above + ru[p, 2, q].astype(F32)).astype(BF16)
            send_up(3, q)
            return carry

        lax.fori_loop(0, F, near, 0)
        x = 2 + p

        def last(q, carry):
            own = nn_dot(dmf[...], dense[0, q])
            done(rd.at[p, H - 1, q], rdr.at[p, H - 1, q])
            done(ru.at[p, H - 1, q], rur.at[p, H - 1, q])
            own = own + rd[p, H - 1, q].astype(F32) + ru[p, H - 1, q].astype(F32)
            pst[x, q] = own.astype(BF16)
            for a in far_first:
                rr = lax.rem(r + a, R)
                if p == 0:
                    dst, sem, to, mine = ebuf.at[2, r, f], xr.at[2, r, f], (behind, rr, q), (r == 0) & (q == f)
                else:
                    dst, sem, to, mine = fin.at[r, q], xr.at[3, r, q], (behind, rr, f), r == 0

                def away():
                    remote(pst.at[x, q], dst, xs.at[x, a, q], sem, to).start()

                if a:
                    away()
                else:
                    pl.when(mine)(lambda: local(pst.at[x, q], dst, sem).start())
                    pl.when(jnp.logical_not(mine))(away)
            return carry

        lax.fori_loop(0, F, last, 0)
        grad_spread(p)

    forward(0)
    mix_one = gathered(0)
    mix[0] = mix_one
    z_one = nn_dot(wt[0], mix_one)
    z1[...] = z_one
    h_one = (z_one / (1.0 + jnp.exp(-z_one))).astype(BF16)
    spread(0, h_one, None, None)
    forward(1)
    mix_two = gathered(1)
    mix[1] = mix_two
    z_two = nn_dot(wt[1], mix_two)
    dz_two = (cot_ref[...].astype(F32) * slope_of(z_two)).astype(BF16)
    spread(1, nn_dot(w2[...], dz_two).astype(BF16), dmb.at[0], dmr.at[0])
    grad_start(0, nt_dot(mix[1], dz_two))
    transposed(0)
    dh_one = gathered(2)
    dz_one = (dh_one.astype(F32) * slope_of(z1[...])).astype(BF16)
    spread(2, nn_dot(w1[...], dz_one).astype(BF16), dmb.at[1], dmr.at[1])
    grad_start(1, nt_dot(mix[0], dz_one))
    transposed(1)
    for a in range(R):
        for q in range(F):
            done(fin.at[a, q], xr.at[3, a, q])
    for q in range(F):
        total = fin[0, q].astype(F32)
        for a in range(1, R):
            total = total + fin[a, q].astype(F32)
        out_ref[:, q * C:(q + 1) * C] = total.astype(BF16)

    grad_end(0, g2_ref)
    grad_end(1, g1_ref)

    one = pst.at[0, 0]

    for q in range(F):
        for n in range(2):
            done(one, p0s.at[q, n])
            done(one, h0s.at[q, n])
        pl.when(r != 0)(functools.partial(done, one, p0s.at[q, 2]))
        pl.when(jnp.logical_not((r == 0) & (f == q)))(functools.partial(done, one, h0s.at[q, 2]))

    for p in range(2):
        def sent_chunk(n, carry):
            s, q = lax.div(n, F), lax.rem(n, F)

            @pl.when((s < 2) | (q < half))
            def _():
                done(one, fs.at[p, s, q])

            @pl.when((s < 2) | (q >= half))
            def _():
                done(one, bs.at[p, s, q])

            return carry

        lax.fori_loop(0, 3 * F, sent_chunk, 0)

        def sent_sum(n, carry):
            s, q = lax.div(n, F), lax.rem(n, F)

            @pl.when((s != 1) | (q < half))
            def _():
                done(one, ds.at[p, s, q])

            @pl.when((s != 1) | (q >= half))
            def _():
                done(one, us.at[p, s, q])

            return carry

        lax.fori_loop(0, 4 * F, sent_sum, 0)
        piece = gsum.at[0]
        for m in range(1, S):
            done(piece, gus.at[p, m])
        for a in range(R):
            for b in range(F):
                if (a, b) != (0, 0):
                    done(piece, gss.at[p, a, b])
                    done(piece, gas.at[p, a, b])
    for a in range(R):
        for b in range(F):
            if (a, b) != (0, 0):
                done(one, xs.at[0, a, b])
                done(one, xs.at[1, a, b])
            if a:
                done(one, xs.at[2, a, b])
                done(one, xs.at[3, a, b])

    for b in range(F):
        pl.when(jnp.logical_not((r == 0) & (f == b)))(functools.partial(done, one, xs.at[2, 0, b]))
        pl.when(r != 0)(functools.partial(done, one, xs.at[3, 0, b]))
        pl.when(f != b)(functools.partial(done, one, ls.at[1, b]))
        pl.when(f != b)(functools.partial(done, one, ls.at[2, b]))


def shards(features, tile_values, tile_coords, section_counts, weight_one, weight_two, cotangent):
    L, R, F = (lax.axis_size(n) for n in ("loop", "rep", "feat"))
    S = L // R
    H = S // 2
    d, nodes = features.shape
    D = weight_one.shape[0]
    C = nodes // F
    piece = D // (R * F)
    dense = dense_sections(tile_values, tile_coords, section_counts, F, nodes)
    scale = 1.0 / math.sqrt(nodes * L)
    vmem = pl.BlockSpec(memory_space=pltpu.VMEM)
    dma = pltpu.SemaphoreType.DMA
    input_grad, g1, g2 = pl.pallas_call(
        functools.partial(layers_kernel, (L, R, F), scale),
        out_shape=(
            jax.ShapeDtypeStruct((d, nodes), BF16),
            jax.ShapeDtypeStruct((D, D), F32),
            jax.ShapeDtypeStruct((D, D), F32),
        ),
        in_specs=[vmem] * 5,
        out_specs=(vmem,) * 3,
        scratch_shapes=[
            pltpu.VMEM((2, S, F, d, C), BF16),
            pltpu.VMEM((d, nodes), F32),
            pltpu.VMEM((4, F, d, C), BF16),
            pltpu.VMEM((3, R, F, d, C), BF16),
            pltpu.VMEM((R, F, d, C), BF16),
            pltpu.VMEM((3, F, d, C), BF16),
            pltpu.VMEM((2, F, d, C), BF16),
            pltpu.VMEM((d, nodes), BF16),
            pltpu.VMEM((D, C), F32),
            pltpu.VMEM((2, D, C), BF16),
        ]
        + [pltpu.VMEM((2, H, F, d, C), BF16)] * 4
        + [
            pltpu.VMEM((2, D, D), BF16),
            pltpu.VMEM((2, R, F, piece, D), F32),
            pltpu.VMEM((2, R, F, piece, D), F32),
            pltpu.VMEM((2, S, piece, D), F32),
            pltpu.VMEM((2, piece, D), F32),
            pltpu.VMEM((2, R, F, piece, D), F32),
            dma((2, R, F)), dma((2, R, F)), dma((2, S)), dma((2, S)), dma((2, R, F)), dma((2, R, F)),
            dma((2, S, F)), dma((2, 3, F)), dma((2, 3, F)),
            dma((4, R, F)), dma((4, R, F)), dma((3, F)), dma((2, F)), dma((F, 3)), dma((F, 3)),
            dma((2, H, F)), dma((2, H, F)), dma((2, H, F)), dma((2, H, F)),
        ],
        compiler_params=pltpu.CompilerParams(
            collective_id=0, has_side_effects=True, vmem_limit_bytes=24 * 1024 * 1024
        ),
        name="layers",
    )(features, dense, weight_one, weight_two, cotangent)
    return (g1, g2, input_grad)


def solution(mesh):
    return jax.shard_map(
        shards,
        mesh=mesh,
        in_specs=(
            P("feat", "loop"),
            P("loop", "rep", None, None, None),
            P("loop", "rep", None, None),
            P("loop", "rep", None),
            P(),
            P(),
            P(None, ("loop", "feat")),
        ),
        out_specs=(P(), P(), P("feat", "loop")),
        check_vma=False,
    )
```

```python
import functools
import math

import jax
import jax.numpy as jnp
from jax import lax
from jax.experimental import pallas as pl
from jax.experimental.pallas import tpu as pltpu
from jax.sharding import PartitionSpec as P

MESH = pl.DeviceIdType.MESH
BF16 = jnp.bfloat16
F32 = jnp.float32


def place_kernel(coords_hbm, counts_hbm, tiles_hbm, out, coords, counts, tiles, sems):
    pairs = ((coords_hbm, coords), (counts_hbm, counts), (tiles_hbm.at[0, 0], tiles))
    copies = [pltpu.make_async_copy(src, dst, sems.at[n]) for n, (src, dst) in enumerate(pairs)]
    for copy in copies:
        copy.start()
    slots, side = tiles.shape[:2]
    sections = out.shape[0]
    per_chunk = out.shape[-1] // side

    def clear(n, carry):
        out[n] = jnp.zeros(out.shape[1:], out.dtype)
        return carry

    lax.fori_loop(0, sections, clear, 0)
    for copy in copies:
        copy.wait()

    def one_section(section, start):
        end = jnp.minimum(start + counts[0, 0, section], slots)

        def one_tile(slot, carry):
            row = pl.multiple_of(coords[0, 0, 0, slot] * side, side)
            col = coords[0, 0, 1, slot]
            lane = pl.multiple_of(lax.rem(col, per_chunk) * side, side)
            out[section, lax.div(col, per_chunk), pl.ds(row, side), pl.ds(lane, side)] = tiles[slot]
            return carry

        lax.fori_loop(start, end, one_tile, 0)
        return end

    lax.fori_loop(0, sections, one_section, 0)


def dense_sections(tile_values, tile_coords, section_counts, chunks, nodes):
    sections = section_counts.shape[-1]
    hbm = pl.BlockSpec(memory_space=pltpu.HBM)
    return pl.pallas_call(
        place_kernel,
        out_shape=jax.ShapeDtypeStruct((sections, chunks, nodes, nodes // chunks), BF16),
        in_specs=[hbm] * 3,
        out_specs=pl.BlockSpec(memory_space=pltpu.VMEM),
        scratch_shapes=[
            pltpu.SMEM(tile_coords.shape, jnp.int32),
            pltpu.SMEM(section_counts.shape, jnp.int32),
            pltpu.VMEM(tile_values.shape[2:], BF16),
            pltpu.SemaphoreType.DMA((3,)),
        ],
        compiler_params=pltpu.CompilerParams(vmem_limit_bytes=8 * 1024 * 1024),
        name="place_tiles",
    )(*(pltpu.with_memory_space_constraint(a, pltpu.HBM) for a in (tile_coords, section_counts, tile_values)))


def nt_dot(a, b):
    return lax.dot_general(a, b, (((1,), (1,)), ((), ())), preferred_element_type=F32)


def nn_dot(a, b):
    return lax.dot_general(a, b, (((1,), (0,)), ((), ())), preferred_element_type=F32)


def slope_of(z):
    s = 1.0 / (1.0 + jnp.exp(-z))
    return s * (1.0 + z * (1.0 - s))


def layers_kernel(
    sizes, scale,
    feat_ref, dense, w1, w2, cot_ref,
    out_ref, g1_ref, g2_ref,
    hbuf, acc, pst, ebuf, fin, lst, dmb, dmf, z1, mix, rd, ru, sd, su, wt, gst, gin, gring, gsum, gall,
    gss, gsr, gus, grr, gas, gar, ringr, fs, bs, xs, xr, ls, dmr, p0s, h0s, rdr, rur, ds, us,
):
    L, R, F = sizes
    S = L // R
    H = S // 2
    half = F // 2
    far_first = sorted(range(R), key=lambda a: -min(a, R - a))
    C = hbuf.shape[-1]
    i, r, f = lax.axis_index("loop"), lax.axis_index("rep"), lax.axis_index("feat")

    def at_loop(value):
        return lax.rem(value + 2 * L, L)

    up, dn = at_loop(i + R), at_loop(i - R)
    up2, dn2 = at_loop(i + 2 * R), at_loop(i - 2 * R)
    ahead, behind = at_loop(i + r), at_loop(i - r)
    block, me = lax.div(i, R), lax.rem(i, R)
    first_of_block = block * R

    def local(src, dst, sem):
        return pltpu.make_async_copy(src, dst, sem)

    def remote(src, dst, ssem, rsem, to):
        return pltpu.make_async_remote_copy(
            src_ref=src, dst_ref=dst, send_sem=ssem, recv_sem=rsem,
            device_id=to, device_id_type=MESH,
        )

    def done(ref, sem):
        pltpu.make_async_copy(ref, ref, sem).wait()

    barrier = pltpu.get_barrier_semaphore()

    def greet(*to):
        pl.semaphore_signal(barrier, inc=1, device_id=to, device_id_type=MESH)

    for m in range(1, S):
        greet(at_loop(i + m * R), r, f)
    for a in range(R):
        for b in range(F):
            if (a, b) != (0, 0):
                greet(i, lax.rem(r + a, R), lax.rem(f + b, F))

    @pl.when(r != 0)
    def _():
        for b in range(F):
            greet(behind, r, b)

    for a in range(1, R):
        for b in range(F):
            greet(at_loop(i + a), a, b)
    for a in range(1, R):
        for b in range(F):
            greet(first_of_block + lax.rem(me + a, R), r, b)
    zero = jnp.zeros(rd.shape[3:], BF16)
    for p in range(2):
        for q in range(F):
            if q >= half:
                rd[p, 1, q] = zero
            else:
                ru[p, 1, q] = zero
    wt[0] = w1[...].T
    wt[1] = w2[...].T
    pl.semaphore_wait(barrier, S - 1 + R * F - 1 + (R - 1) * F + jnp.where(r != 0, F + R * F, 0))

    def to_ring(p, src, q, ssem, ff):
        mine = (r == 0) & (ff == f)

        @pl.when(mine)
        def _():
            local(src, hbuf.at[p, 0, q], ringr.at[p, 0, q]).start()

        @pl.when(jnp.logical_not(mine))
        def _():
            remote(src, hbuf.at[p, 0, q], ssem, ringr.at[p, 0, q], (ahead, r, ff)).start()

    for q in range(F):
        to_ring(0, feat_ref.at[:, pl.ds(q * C, C)], q, p0s.at[q], f)

    def forward(p):
        def hop(k, to_k, q, ssem, to):
            remote(hbuf.at[p, k, q], hbuf.at[p, to_k, q], ssem, ringr.at[p, to_k, q], (to, r, f)).start()

        def here(k, q):
            done(hbuf.at[p, k, q], ringr.at[p, k, q])

        def term(k, q):
            return nt_dot(hbuf[p, k, q], dense[k, q])

        def first(q, carry):
            here(0, q)
            hop(0, 1, q, fs.at[p, 0, q], up)
            hop(0, S - 1, q, bs.at[p, 0, q], dn)
            value = term(0, q)

            @pl.when(q == 0)
            def _():
                acc[...] = value

            @pl.when(q != 0)
            def _():
                acc[...] += value

            return carry

        lax.fori_loop(0, F, first, 0)

        def near(q, carry):
            here(1, q)
            hop(1, 2, q, fs.at[p, 1, q], up)
            here(S - 1, q)
            hop(S - 1, S - 2, q, bs.at[p, 1, q], dn)
            acc[...] += term(1, q) + term(S - 1, q)
            return carry

        lax.fori_loop(0, F, near, 0)

        def middle(q, carry):
            here(2, q)

            @pl.when(q < half)
            def _():
                hop(2, H, q, fs.at[p, 3, q], up2)

            hop(2, 3, q, fs.at[p, 2, q], up)
            here(S - 2, q)

            @pl.when(q >= half)
            def _():
                hop(S - 2, H, q, bs.at[p, 3, q], dn2)

            hop(S - 2, S - 3, q, bs.at[p, 2, q], dn)
            acc[...] += term(2, q) + term(S - 2, q)
            return carry

        lax.fori_loop(0, F, middle, 0)

        def far(q, carry):
            here(3, q)
            here(S - 3, q)
            here(H, q)
            acc[...] += term(3, q) + term(S - 3, q) + term(H, q)
            return carry

        lax.fori_loop(0, F, far, 0)
        for q in range(F):
            pst[p, q] = acc[:, q * C:(q + 1) * C].astype(BF16)
        for a in far_first:
            for b in range(F):
                rr, q = lax.rem(r + a, R), lax.rem(f + b, F)
                if (a, b) == (0, 0):
                    local(pst.at[p, q], ebuf.at[p, r, f], xr.at[p, r, f]).start()
                else:
                    remote(pst.at[p, q], ebuf.at[p, r, f], xs.at[p, a, b], xr.at[p, r, f], (i, rr, q)).start()

    def gathered(e):
        total = None
        for a in range(R):
            for b in range(F):
                done(ebuf.at[e, a, b], xr.at[e, a, b])
        for a in range(R):
            part = ebuf[e, a].reshape(z1.shape).astype(F32)
            total = part if total is None else total + part
        return total.astype(BF16)

    def spread(n, value, dst, sem):
        lst[n] = value.reshape(lst.shape[1:])
        for b in range(F):
            ff = lax.rem(f + b, F)
            if n == 0:
                to_ring(1, lst.at[n, ff], f, h0s.at[ff], ff)
            elif b:
                remote(lst.at[n, ff], dst.at[f], ls.at[n, ff], sem.at[f], (i, r, ff)).start()
            else:
                local(lst.at[n, ff], dst.at[f], sem.at[f]).start()

    def grad_start(g, value):
        gst[g] = value.reshape(gst.shape[1:])
        for a in range(R):
            for b in range(F):
                c, ff = lax.rem(me + a, R), lax.rem(f + b, F)
                if (a, b) == (0, 0):
                    local(gst.at[g, r, f], gin.at[g, me, f], gsr.at[g, me, f]).start()
                else:
                    to = (first_of_block + c, r, ff)
                    remote(gst.at[g, r, ff], gin.at[g, me, f], gss.at[g, a, b], gsr.at[g, me, f], to).start()

    def grad_send(g, m):
        slot = gring.at[g, block]
        return remote(slot, slot, gus.at[g, m], grr.at[g, block], (at_loop(i + m * R), r, f))

    def grad_block(g):
        total = None
        for a in range(R):
            for b in range(F):
                done(gin.at[g, a, b], gsr.at[g, a, b])
        for a in range(R):
            for b in range(F):
                total = gin[g, a, b] if total is None else total + gin[g, a, b]
        gring[g, block] = total
        for m in range(1, S):
            grad_send(g, m).start()

    def grad_spread(g):
        for m in range(1, S):
            other = lax.rem(block + m, S)
            done(gring.at[g, other], grr.at[g, other])
        total = gring[g, 0]
        for n in range(1, S):
            total = total + gring[g, n]
        gsum[g] = total * scale
        for a in range(R):
            for b in range(F):
                if (a, b) == (0, 0):
                    local(gsum.at[g], gall.at[g, r, f], gar.at[g, r, f]).start()
                else:
                    to = (i, lax.rem(r + a, R), lax.rem(f + b, F))
                    remote(gsum.at[g], gall.at[g, r, f], gas.at[g, a, b], gar.at[g, r, f], to).start()

    def grad_end(g, ref):
        for a in range(R):
            for b in range(F):
                done(gall.at[g, a, b], gar.at[g, a, b])
        ref[...] = gall[g].reshape(ref.shape)

    def transposed(p):
        for q in range(F):
            done(dmb.at[p, q], dmr.at[p, q])
            dmf[:, q * C:(q + 1) * C] = dmb[p, q]

        def send_dn(s, q, to=dn):
            remote(sd.at[p, s, q], rd.at[p, s, q], ds.at[p, s, q], rdr.at[p, s, q], (to, r, f)).start()

        def send_up(s, q, to=up):
            remote(su.at[p, s, q], ru.at[p, s, q], us.at[p, s, q], rur.at[p, s, q], (to, r, f)).start()

        def term(k, q):
            return nn_dot(dmf[...], dense[k, q])

        def from_dn(s, q):
            done(rd.at[p, s, q], rdr.at[p, s, q])

        def from_up(s, q):
            done(ru.at[p, s, q], rur.at[p, s, q])

        def far(q, carry):
            value = term(H, q).astype(BF16)

            @pl.when(q < half)
            def _():
                sd[p, 1, q] = value
                send_dn(1, q, dn2)

            @pl.when(q >= half)
            def _():
                su[p, 1, q] = value
                send_up(1, q, up2)

            sd[p, 0, q] = term(3, q).astype(BF16)
            send_dn(0, q)
            su[p, 0, q] = term(S - 3, q).astype(BF16)
            send_up(0, q)
            return carry

        lax.fori_loop(0, F, far, 0)

        def middle(q, carry):
            down, above = term(2, q), term(S - 2, q)
            from_dn(0, q)
            pl.when(q < half)(lambda: from_dn(1, q))
            sd[p, 2, q] = (down + rd[p, 0, q].astype(F32) + rd[p, 1, q].astype(F32)).astype(BF16)
            send_dn(2, q)
            from_up(0, q)
            pl.when(q >= half)(lambda: from_up(1, q))
            su[p, 2, q] = (above + ru[p, 0, q].astype(F32) + ru[p, 1, q].astype(F32)).astype(BF16)
            send_up(2, q)
            return carry

        lax.fori_loop(0, F, middle, 0)
        grad_block(p)

        def near(q, carry):
            down, above = term(1, q), term(S - 1, q)
            from_dn(2, q)
            sd[p, 3, q] = (down + rd[p, 2, q].astype(F32)).astype(BF16)
            send_dn(3, q)
            from_up(2, q)
            su[p, 3, q] = (above + ru[p, 2, q].astype(F32)).astype(BF16)
            send_up(3, q)
            return carry

        lax.fori_loop(0, F, near, 0)
        x = 2 + p

        def last(q, carry):
            own = nn_dot(dmf[...], dense[0, q])
            done(rd.at[p, H - 1, q], rdr.at[p, H - 1, q])
            done(ru.at[p, H - 1, q], rur.at[p, H - 1, q])
            own = own + rd[p, H - 1, q].astype(F32) + ru[p, H - 1, q].astype(F32)
            pst[x, q] = own.astype(BF16)
            for a in far_first:
                rr = lax.rem(r + a, R)
                if p == 0:
                    dst, sem, to, mine = ebuf.at[2, r, f], xr.at[2, r, f], (behind, rr, q), (r == 0) & (q == f)
                else:
                    dst, sem, to, mine = fin.at[r, q], xr.at[3, r, q], (behind, rr, f), r == 0

                def away():
                    remote(pst.at[x, q], dst, xs.at[x, a, q], sem, to).start()

                if a:
                    away()
                else:
                    pl.when(mine)(lambda: local(pst.at[x, q], dst, sem).start())
                    pl.when(jnp.logical_not(mine))(away)
            return carry

        lax.fori_loop(0, F, last, 0)
        grad_spread(p)

    forward(0)
    mix_one = gathered(0)
    mix[0] = mix_one
    z_one = nn_dot(wt[0], mix_one)
    z1[...] = z_one
    h_one = (z_one / (1.0 + jnp.exp(-z_one))).astype(BF16)
    spread(0, h_one, None, None)
    forward(1)
    mix_two = gathered(1)
    mix[1] = mix_two
    z_two = nn_dot(wt[1], mix_two)
    dz_two = (cot_ref[...].astype(F32) * slope_of(z_two)).astype(BF16)
    spread(1, nn_dot(w2[...], dz_two).astype(BF16), dmb.at[0], dmr.at[0])
    grad_start(0, nt_dot(mix[1], dz_two))
    transposed(0)
    dh_one = gathered(2)
    dz_one = (dh_one.astype(F32) * slope_of(z1[...])).astype(BF16)
    spread(2, nn_dot(w1[...], dz_one).astype(BF16), dmb.at[1], dmr.at[1])
    grad_start(1, nt_dot(mix[0], dz_one))
    transposed(1)
    one = pst.at[0, 0]

    for q in range(F):
        pl.when(jnp.logical_not((r == 0) & (f == q)))(functools.partial(done, one, h0s.at[q]))

        @pl.when(r != 0)
        def _():
            done(one, p0s.at[q])

    for p in range(2):
        def sent_chunk(n, carry):
            s, q = lax.div(n, F), lax.rem(n, F)

            @pl.when((s < 3) | (q < half))
            def _():
                done(one, fs.at[p, s, q])

            @pl.when((s < 3) | (q >= half))
            def _():
                done(one, bs.at[p, s, q])

            return carry

        lax.fori_loop(0, 4 * F, sent_chunk, 0)

        def sent_sum(n, carry):
            s, q = lax.div(n, F), lax.rem(n, F)

            @pl.when((s != 1) | (q < half))
            def _():
                done(one, ds.at[p, s, q])

            @pl.when((s != 1) | (q >= half))
            def _():
                done(one, us.at[p, s, q])

            return carry

        lax.fori_loop(0, 4 * F, sent_sum, 0)
        piece = gsum.at[0]
        for m in range(1, S):
            done(piece, gus.at[p, m])
        for a in range(R):
            for b in range(F):
                if (a, b) != (0, 0):
                    done(piece, gss.at[p, a, b])
                    done(piece, gas.at[p, a, b])
    for a in range(R):
        for b in range(F):
            if (a, b) != (0, 0):
                done(one, xs.at[0, a, b])
                done(one, xs.at[1, a, b])
            if a:
                done(one, xs.at[2, a, b])
                done(one, xs.at[3, a, b])

    for b in range(F):
        pl.when(jnp.logical_not((r == 0) & (f == b)))(functools.partial(done, one, xs.at[2, 0, b]))
        pl.when(r != 0)(functools.partial(done, one, xs.at[3, 0, b]))
        pl.when(f != b)(functools.partial(done, one, ls.at[1, b]))
        pl.when(f != b)(functools.partial(done, one, ls.at[2, b]))

    for a in range(R):
        for q in range(F):
            done(fin.at[a, q], xr.at[3, a, q])
    for q in range(F):
        total = fin[0, q].astype(F32)
        for a in range(1, R):
            total = total + fin[a, q].astype(F32)
        out_ref[:, q * C:(q + 1) * C] = total.astype(BF16)

    grad_end(0, g2_ref)
    grad_end(1, g1_ref)


def shards(features, tile_values, tile_coords, section_counts, weight_one, weight_two, cotangent):
    L, R, F = (lax.axis_size(n) for n in ("loop", "rep", "feat"))
    S = L // R
    H = S // 2
    d, nodes = features.shape
    D = weight_one.shape[0]
    C = nodes // F
    piece = D // (R * F)
    dense = dense_sections(tile_values, tile_coords, section_counts, F, nodes)
    scale = 1.0 / math.sqrt(nodes * L)
    vmem = pl.BlockSpec(memory_space=pltpu.VMEM)
    dma = pltpu.SemaphoreType.DMA
    input_grad, g1, g2 = pl.pallas_call(
        functools.partial(layers_kernel, (L, R, F), scale),
        out_shape=(
            jax.ShapeDtypeStruct((d, nodes), BF16),
            jax.ShapeDtypeStruct((D, D), F32),
            jax.ShapeDtypeStruct((D, D), F32),
        ),
        in_specs=[vmem] * 5,
        out_specs=(vmem,) * 3,
        scratch_shapes=[
            pltpu.VMEM((2, S, F, d, C), BF16),
            pltpu.VMEM((d, nodes), F32),
            pltpu.VMEM((4, F, d, C), BF16),
            pltpu.VMEM((3, R, F, d, C), BF16),
            pltpu.VMEM((R, F, d, C), BF16),
            pltpu.VMEM((3, F, d, C), BF16),
            pltpu.VMEM((2, F, d, C), BF16),
            pltpu.VMEM((d, nodes), BF16),
            pltpu.VMEM((D, C), F32),
            pltpu.VMEM((2, D, C), BF16),
        ]
        + [pltpu.VMEM((2, H, F, d, C), BF16)] * 4
        + [
            pltpu.VMEM((2, D, D), BF16),
            pltpu.VMEM((2, R, F, piece, D), F32),
            pltpu.VMEM((2, R, F, piece, D), F32),
            pltpu.VMEM((2, S, piece, D), F32),
            pltpu.VMEM((2, piece, D), F32),
            pltpu.VMEM((2, R, F, piece, D), F32),
            dma((2, R, F)), dma((2, R, F)), dma((2, S)), dma((2, S)), dma((2, R, F)), dma((2, R, F)),
            dma((2, S, F)), dma((2, 4, F)), dma((2, 4, F)),
            dma((4, R, F)), dma((4, R, F)), dma((3, F)), dma((2, F)), dma((F,)), dma((F,)),
            dma((2, H, F)), dma((2, H, F)), dma((2, H, F)), dma((2, H, F)),
        ],
        compiler_params=pltpu.CompilerParams(
            collective_id=0, has_side_effects=True, vmem_limit_bytes=24 * 1024 * 1024
        ),
        name="layers",
    )(features, dense, weight_one, weight_two, cotangent)
    return (g1, g2, input_grad)


def solution(mesh):
    return jax.shard_map(
        shards,
        mesh=mesh,
        in_specs=(
            P("feat", "loop"),
            P("loop", "rep", None, None, None),
            P("loop", "rep", None, None),
            P("loop", "rep", None),
            P(),
            P(),
            P(None, ("loop", "feat")),
        ),
        out_specs=(P(), P(), P("feat", "loop")),
        check_vma=False,
    )
```
